32 devices in a mesh: seq: 16 (over z, y, x), head: 2 (over core).
Axes of the slice: x: 2, y: 2, z: 4, core: 2. Of those that a mesh axis runs over, the one named last changes fastest.
Arguments:
- tokens: bfloat16 [16, 1024, 3072], P('seq', None, 'head'), may hold values from -6 to 6
- fast_state: float32 [16, 8, 192, 2304], P('seq', 'head'), may hold values from -6 to 6
- momentum: float32 [16, 8, 192, 2304], P('seq', 'head'), may hold values from -1.8 to 1.8
- init_fast: bfloat16 [8, 192, 2304], P('head'), may hold values from -6 to 6
- past_keys: bfloat16 [16, 2048, 1536], P('seq', None, 'head'), may hold values from -6 to 6
- past_values: bfloat16 [16, 2048, 1536], P('seq', None, 'head'), may hold values from -6 to 6
- qkv_weight: bfloat16 [3, 3072, 1536], P(None, 'seq', 'head'), may hold values from -0.109375 to 0.109375
- rate_weight: bfloat16 [3072, 8], P(None, 'head'), may hold values from -0.109375 to 0.109375
- out_weight: bfloat16 [1536, 3072], P('head'), may hold values from -0.15625 to 0.15625
- prompt_begins: int32 [2, 16], replicated, may hold values 0 or 1
Outputs:
- mixed: bfloat16 [16, 1024, 3072], P('seq', None, 'head')
- fast_out: float32 [16, 8, 192, 2304], P('seq', 'head')
- momentum_out: float32 [16, 8, 192, 2304], P('seq', 'head')
The draws below stay inside these ranges and needn't reach their ends.
All inputs are finite; a program needn't handle non-finite values.
Results may differ from the reference program's by a relative error of at most 0.015.
Values may be sent and summed in bfloat16 or wider, within the bound.
A program may use at most 192 MiB of HBM per device.

```python
import math
import jax
import jax.numpy as jnp
from jax import lax

D = 3072
HEADS = 8
HD = 192
HID = 768
SPAN = 512
WINDOW = 2048
STEPS = 2
POSITIONS = 16
N_HEAD = 2


def plant(drawn, own_key, low, top_value):
    longest = drawn.shape.index(max(drawn.shape))
    spots = []
    for shift in (0, 1):
        where = [jax.random.randint(jax.random.fold_in(own_key, axis), (), 0, length) for axis, length in enumerate(drawn.shape)]
        where[longest] = (where[longest] + shift) % drawn.shape[longest]
        spots.append(tuple(where))
    return drawn.at[spots[0]].set(low).at[spots[1]].set(top_value)


def block_levels(own_key, extent, pieces, least, top_value):
    def one(position, shards_of):
        steps = jax.random.uniform(jax.random.fold_in(jax.random.fold_in(own_key, 6), position), (shards_of,), jnp.float32, least / len(pieces), top_value / len(pieces))
        return jnp.repeat(jnp.exp(steps), extent[position] // shards_of).reshape((-1,) + (1,) * (len(extent) - position - 1))

    loudness = one(*pieces[0])
    for cut in pieces[1:]:
        loudness = loudness * one(*cut)
    return loudness


def noise(stream_key, shape, width, reach, cuts=(), kind=jnp.bfloat16):
    values = jax.random.normal(stream_key, shape, jnp.float32) * width
    if len(cuts) > 0:
        values = block_levels(stream_key, shape, cuts, -0.22, 0.18) * values
    return jnp.clip(values, min=-reach, max=reach).astype(kind)


def setup_inputs(seed: int = 0) -> dict:
    arg_keys = jax.random.split(jax.random.key(seed), 11)
    tokens = noise(arg_keys[0], (POSITIONS, STEPS * SPAN, D), 1.0, 6.0, ((0, 16), (2, 2)))
    fast_state = noise(arg_keys[1], (POSITIONS, HEADS, HD, 3 * HID), 1.0, 6.0, ((0, 16), (1, 2)), jnp.float32)
    momentum = noise(arg_keys[2], (POSITIONS, HEADS, HD, 3 * HID), 0.3, 1.8, ((0, 16), (1, 2)), jnp.float32)
    init_fast = noise(arg_keys[3], (HEADS, HD, 3 * HID), 1.0, 6.0, ((0, 2),))
    past_keys = noise(arg_keys[4], (POSITIONS, WINDOW, HEADS * HD), 1.0, 6.0, ((0, 16), (2, 2)))
    past_values = noise(arg_keys[5], (POSITIONS, WINDOW, HEADS * HD), 1.0, 6.0, ((0, 16), (2, 2)))
    qkv_weight = noise(arg_keys[6], (3, D, HEADS * HD), D ** -0.5, 0.109375, ((1, 16), (2, 2)))
    rate_weight = noise(arg_keys[7], (D, HEADS), D ** -0.5, 0.109375, ((1, 2),))
    out_weight = noise(arg_keys[8], (HEADS * HD, D), (HEADS * HD) ** -0.5, 0.15625, ((0, 2),))
    prompt_begins = plant((jax.random.randint(arg_keys[9], (STEPS, POSITIONS), 0, 4) < 1).astype(jnp.int32), jax.random.fold_in(arg_keys[9], 1), 0, 1)
    return dict(tokens=tokens, fast_state=fast_state, momentum=momentum, init_fast=init_fast, past_keys=past_keys, past_values=past_values, qkv_weight=qkv_weight, rate_weight=rate_weight, out_weight=out_weight, prompt_begins=prompt_begins)


momentum_decay = 0.9
rate_scale = 0.3
epsilon = 1e-06
highest = lax.Precision.HIGHEST

def unit_rows(matrix):
    return matrix * lax.rsqrt(lax.optimization_barrier(jnp.mean(matrix * matrix, axis=-1, keepdims=True)) + epsilon)

def head_span(queries, keys_span, values_span, step_size, window_keys, window_values, visible_prev, restart, weights_now, momentum_now, initial):
    span_len = queries.shape[0]
    window_len = window_keys.shape[0]
    head_dim = queries.shape[1]
    hidden = weights_now.shape[1] // 3
    score_bound = math.sqrt(head_dim)
    query_unit = unit_rows(queries.astype(jnp.float32))
    key_unit = unit_rows(keys_span.astype(jnp.float32))
    context_keys = jnp.concatenate([unit_rows(window_keys.astype(jnp.float32)), key_unit], axis=0).astype(jnp.bfloat16)
    context_values = jnp.concatenate([window_values, values_span], axis=0)
    scores = lax.dot_general(query_unit.astype(jnp.bfloat16), context_keys, (((1,), (1,)), ((), ())), preferred_element_type=jnp.float32) / score_bound
    query_pos = lax.broadcasted_iota(jnp.int32, scores.shape, 0)
    key_pos = lax.broadcasted_iota(jnp.int32, scores.shape, 1)
    restart_flag = restart.astype(jnp.float32)
    keep_prev = jnp.concatenate([visible_prev * (1.0 - restart_flag), jnp.ones((span_len,), jnp.float32)])
    inside = (key_pos > query_pos) & (key_pos <= query_pos + window_len)
    soft_weights = jnp.where(inside, jnp.exp(scores - score_bound), 0.0) * keep_prev[None, :]
    denominator = lax.optimization_barrier(jnp.sum(soft_weights, axis=1, keepdims=True))
    attended = jnp.dot(soft_weights.astype(jnp.bfloat16), context_values, preferred_element_type=jnp.float32) / denominator
    weights_now = jnp.where(restart > 0, initial.astype(jnp.float32), weights_now)
    momentum_now = jnp.where(restart > 0, jnp.zeros_like(momentum_now), momentum_now)
    up_proj = weights_now[:, :2 * hidden]
    down_proj = weights_now[:, 2 * hidden:]
    hidden_scale = math.sqrt(hidden)
    query_in = query_unit / score_bound
    key_in = key_unit / score_bound
    both_in = jnp.dot(query_in, up_proj, precision=highest, preferred_element_type=jnp.float32)
    mixed_hidden = jax.nn.silu(both_in[:, :hidden]) * both_in[:, hidden:]
    applied = lax.dot_general(mixed_hidden, down_proj, (((1,), (1,)), ((), ())), precision=highest, preferred_element_type=jnp.float32) / hidden_scale
    both_key = jnp.dot(key_in, up_proj, precision=highest, preferred_element_type=jnp.float32)
    gate_key = both_key[:, :hidden]
    lift_key = both_key[:, hidden:]
    gate_sigmoid = jax.nn.sigmoid(gate_key)
    gate_silu = gate_key * gate_sigmoid
    hidden_key = gate_silu * lift_key
    out_grad = -step_size.astype(jnp.float32)[:, None] * values_span.astype(jnp.float32)
    down_grad = lax.dot_general(out_grad, hidden_key, (((0,), (0,)), ((), ())), precision=highest, preferred_element_type=jnp.float32) / hidden_scale
    hidden_grad = jnp.dot(out_grad, down_proj, precision=highest, preferred_element_type=jnp.float32) / hidden_scale
    gate_grad = hidden_grad * lift_key * gate_sigmoid * (1.0 + gate_key * (1.0 - gate_sigmoid))
    lift_grad = hidden_grad * gate_silu
    up_grad = lax.dot_general(key_in, jnp.concatenate([gate_grad, lift_grad], axis=1), (((0,), (0,)), ((), ())), precision=highest, preferred_element_type=jnp.float32)
    gradient = jnp.concatenate([up_grad, down_grad], axis=1)
    momentum_new = momentum_decay * momentum_now + gradient
    stepped = weights_now - momentum_new
    weights_new = stepped * lax.rsqrt(lax.optimization_barrier(jnp.mean(stepped * stepped, axis=0, keepdims=True)) + epsilon)
    head_mix = (attended + applied).astype(jnp.bfloat16)
    return (head_mix, weights_new, momentum_new)

def position_span(queries, keys_span, values_span, step_size, window_keys, window_values, visible_prev, restart, weights_now, momentum_now, initial):
    heads_here = weights_now.shape[0]

    def split_heads(matrix):
        return matrix.reshape(matrix.shape[0], heads_here, matrix.shape[1] // heads_here)
    mapped = jax.vmap(head_span, in_axes=(1, 1, 1, 1, 1, 1, None, None, 0, 0, 0), out_axes=(1, 0, 0))
    head_mix, weights_new, momentum_new = mapped(split_heads(queries), split_heads(keys_span), split_heads(values_span), step_size, split_heads(window_keys), split_heads(window_values), visible_prev, restart, weights_now, momentum_now, initial)
    return (head_mix.reshape(head_mix.shape[0], -1), weights_new, momentum_new)

def next_window(window_keys, window_values, visible_prev, restart, keys_span, values_span):
    window_len = window_keys.shape[0]
    kept_rows = visible_prev * (1.0 - restart.astype(visible_prev.dtype))
    fresh_rows = jnp.ones((keys_span.shape[0],), visible_prev.dtype)
    new_keys = jnp.concatenate([window_keys, keys_span], axis=0)[-window_len:]
    new_values = jnp.concatenate([window_values, values_span], axis=0)[-window_len:]
    new_visible = jnp.concatenate([kept_rows, fresh_rows])[-window_len:]
    return (new_keys, new_values, new_visible)

def reference(tokens, fast_state, momentum, init_fast, past_keys, past_values, qkv_weight, rate_weight, out_weight, prompt_begins):
    positions = tokens.shape[0]

    def project(token_rows):
        query_all = jnp.dot(token_rows, qkv_weight[0], preferred_element_type=jnp.float32).astype(jnp.bfloat16)
        key_all = jnp.dot(token_rows, qkv_weight[1], preferred_element_type=jnp.float32).astype(jnp.bfloat16)
        value_all = jnp.dot(token_rows, qkv_weight[2], preferred_element_type=jnp.float32).astype(jnp.bfloat16)
        rates = (rate_scale * jax.nn.softplus(jnp.dot(token_rows, rate_weight, preferred_element_type=jnp.float32))).astype(jnp.bfloat16)
        return (query_all, key_all, value_all, rates)
    queries, keys_all, values_all, step_sizes = lax.map(project, tokens)
    weights_now = fast_state
    momentum_now = momentum
    window_keys = past_keys
    window_values = past_values
    visible = jnp.ones((positions, WINDOW), jnp.float32)
    mix_blocks = []

    def one_position(packed):
        return position_span(*packed, init_fast)
    for section_index in range(STEPS):
        first_row = section_index * SPAN
        last_row = first_row + SPAN
        restart = prompt_begins[section_index]
        span_keys = keys_all[:, first_row:last_row]
        span_values = values_all[:, first_row:last_row]
        head_mix, weights_new, momentum_new = lax.map(one_position, (queries[:, first_row:last_row], span_keys, span_values, step_sizes[:, first_row:last_row], window_keys, window_values, visible, restart, weights_now, momentum_now))
        window_keys, window_values, visible = jax.vmap(next_window)(window_keys, window_values, visible, restart, span_keys, span_values)
        mix_blocks.append(head_mix)
        if section_index + 1 < STEPS:
            weights_now = jnp.roll(weights_new, 1, axis=0)
            momentum_now = jnp.roll(momentum_new, 1, axis=0)
            window_keys = jnp.roll(window_keys, 1, axis=0)
            window_values = jnp.roll(window_values, 1, axis=0)
            visible = jnp.roll(visible, 1, axis=0)
        else:
            weights_now = weights_new
            momentum_now = momentum_new
    head_rows_all = jnp.concatenate(mix_blocks, axis=1)
    group_width = HEADS // N_HEAD * HD

    def project_out(head_rows):
        running = jnp.zeros((head_rows.shape[0], out_weight.shape[1]), jnp.float32)
        for group_index in range(N_HEAD):
            lower = group_index * group_width
            partial_value = jnp.dot(head_rows[:, lower:lower + group_width], out_weight[lower:lower + group_width], preferred_element_type=jnp.float32).astype(jnp.bfloat16)
            partial_value = lax.optimization_barrier(partial_value)
            running = running + partial_value.astype(jnp.float32)
        return running.astype(jnp.bfloat16)
    mixed = lax.map(project_out, head_rows_all)
    return (mixed, weights_now, momentum_now)
```

```python
import functools
import math

import jax
import jax.numpy as jnp
from jax import lax
from jax.experimental import pallas as pl
from jax.experimental.pallas import tpu as pltpu
from jax.sharding import PartitionSpec as P

momentum_decay = 0.9
rate_scale = 0.3
epsilon = 1e-06
f32 = jnp.float32
bf16 = jnp.bfloat16


def passed_along(block, axis, distance):
    n = lax.axis_size(axis)
    return lax.ppermute(block, axis, [((i - distance) % n, i) for i in range(n)])


def unit_rows(matrix):
    matrix = matrix.astype(f32)
    return matrix * lax.rsqrt(jnp.mean(matrix * matrix, axis=-1, keepdims=True) + epsilon)


def mm(a, b, ca, cb):
    return lax.dot_general(a, b, (((ca,), (cb,)), ((), ())), preferred_element_type=f32)


def fast_kernel(steps, span, begins, q, k, v, rate, fast, mom, init, applied, fast_out, mom_out):
    group, hd, three = fast.shape
    hid = three // 3
    inv_bound = 1.0 / math.sqrt(hd)
    inv_hidden = 1.0 / math.sqrt(hid)
    for h in range(group):
        cols = slice(h * hd, (h + 1) * hd)
        w = fast[h]
        m = mom[h]
        for s in range(steps):
            rows = slice(s * span, (s + 1) * span)
            fresh = begins[s] > 0
            w = jnp.where(fresh, init[h].astype(f32), w)
            m = jnp.where(fresh, 0.0, m)
            wb = w.astype(bf16)
            up = wb[:, : 2 * hid]
            down = wb[:, 2 * hid :]
            xq = (unit_rows(q[rows, cols]) * inv_bound).astype(bf16)
            ab = mm(xq, up, 1, 0)
            a = ab[:, :hid]
            hq = (a * jax.nn.sigmoid(a) * ab[:, hid:]).astype(bf16)
            applied[rows, cols] = mm(hq, down, 1, 1) * inv_hidden
            y = (unit_rows(k[rows, cols]) * inv_bound).astype(bf16)
            ab = mm(y, up, 1, 0)
            a = ab[:, :hid]
            b = ab[:, hid:]
            sg = jax.nn.sigmoid(a)
            act = a * sg
            g = (-rate[rows, h : h + 1] * v[rows, cols].astype(f32)).astype(bf16)
            grad_down = mm(g, (act * b).astype(bf16), 0, 0) * inv_hidden
            e = mm(g, down, 1, 0) * inv_hidden
            da = (e * b * sg * (1.0 + a * (1.0 - sg))).astype(bf16)
            db = (e * act).astype(bf16)
            grad = jnp.concatenate([mm(y, da, 0, 0), mm(y, db, 0, 0), grad_down], axis=1)
            m = momentum_decay * m + grad
            w = w - m
            w = w * lax.rsqrt(jnp.mean(w * w, axis=0, keepdims=True) + epsilon)
        fast_out[h] = w.astype(bf16)
        mom_out[h] = m.astype(bf16)


def attend_kernel(steps, span, hd, begins, q, k, v, past_k, past_v, applied, mix):
    window = past_k.shape[0]
    blocks = window // span
    bound = math.sqrt(hd)
    for h in range(q.shape[1] // hd):
        cols = slice(h * hd, (h + 1) * hd)
        keys = []
        values = []
        ones = jnp.ones((span, 64), bf16)
        for c in range(blocks + steps):
            kr, vr, at = (past_k, past_v, c) if c < blocks else (k, v, c - blocks)
            rows = slice(at * span, (at + 1) * span)
            keys.append(unit_rows(kr[rows, cols]).astype(bf16))
            values.append(jnp.concatenate([vr[rows, cols], ones], axis=1))
        for s in range(steps):
            rows = slice(s * span, (s + 1) * span)
            qn = unit_rows(q[rows, cols]).astype(bf16)
            acc = jnp.zeros((span, hd + 64), f32)
            row = lax.broadcasted_iota(jnp.int32, (span, span), 0)
            col = lax.broadcasted_iota(jnp.int32, (span, span), 1)
            for c in range(s, s + blocks + 1):
                dead = jnp.int32(0)
                for t in range(max(0, c - blocks + 1), s + 1):
                    dead = jnp.maximum(dead, begins[t])
                shift = jnp.where(dead > 0, -1e30, -bound)
                p = jnp.exp(mm(qn, keys[c], 1, 1) * (1.0 / bound) + shift)
                if c == s:
                    p = jnp.where(col > row, p, 0.0)
                if c == s + blocks:
                    p = jnp.where(col <= row, p, 0.0)
                acc = acc + mm(p.astype(bf16), values[c], 1, 0)
            out = acc[:, :hd] / acc[:, hd : hd + 1]
            mix[rows, cols] = (out + applied[rows, cols]).astype(bf16)


def body(
    tokens,
    fast_state,
    momentum,
    init_fast,
    past_keys,
    past_values,
    qkv_weight,
    rate_weight,
    out_weight,
    prompt_begins,
):
    n = lax.axis_size("seq")
    me = lax.axis_index("seq")
    steps = prompt_begins.shape[0]
    total = tokens.shape[1]
    span = total // steps
    window = past_keys.shape[1]
    heads, hd, three = fast_state.shape[1:]
    group = 2 if heads % 2 == 0 else heads
    wide = group * hd

    spans = [tokens[0, :span]]
    for s in range(1, steps):
        spans.append(passed_along(tokens[0, s * span : (s + 1) * span], "seq", -s))
    features = lax.all_gather(jnp.concatenate(spans, axis=0), "head", axis=1, tiled=True)
    weights = lax.all_gather(qkv_weight, "seq", axis=1, tiled=True)
    q, k, v = [
        jnp.dot(features, weights[c], preferred_element_type=f32).astype(bf16) for c in range(3)
    ]
    rates = (
        rate_scale
        * jax.nn.softplus(jnp.dot(features, rate_weight, preferred_element_type=f32))
    ).astype(bf16).astype(f32)
    begins = jnp.stack([prompt_begins[s, (me + s) % n] for s in range(steps)])

    smem = pl.BlockSpec(memory_space=pltpu.SMEM)

    def columns(rows, g):
        return pl.BlockSpec((rows, wide), lambda i, g=g: (0, g))

    def state(g):
        return pl.BlockSpec((None, group, hd, three), lambda i, g=g: (0, g, 0, 0))

    params = pltpu.CompilerParams(vmem_limit_bytes=60000 * 1024)
    applied = []
    sent = []
    for g in range(heads // group):
        a, w, m = pl.pallas_call(
            functools.partial(fast_kernel, steps, span),
            grid=(1,),
            in_specs=[
                smem,
                columns(total, g),
                columns(total, g),
                columns(total, g),
                pl.BlockSpec((None, total, group), lambda i, g=g: (g, 0, 0)),
                state(g),
                state(g),
                pl.BlockSpec((group, hd, three), lambda i, g=g: (g, 0, 0)),
            ],
            out_specs=[
                pl.BlockSpec((total, wide), lambda i: (0, 0)),
                pl.BlockSpec((group, hd, three), lambda i: (0, 0, 0)),
                pl.BlockSpec((group, hd, three), lambda i: (0, 0, 0)),
            ],
            out_shape=[
                jax.ShapeDtypeStruct((total, wide), f32),
                jax.ShapeDtypeStruct((group, hd, three), bf16),
                jax.ShapeDtypeStruct((group, hd, three), bf16),
            ],
            compiler_params=params,
            name=f"fast_{g}",
        )(
            begins,
            q,
            k,
            v,
            rates.reshape(total, heads // group, group).transpose(1, 0, 2),
            fast_state,
            momentum,
            init_fast,
        )
        applied.append(a)
        sent.append((passed_along(w, "seq", steps - 1), passed_along(m, "seq", steps - 1)))

    mixes = []
    for g in range(heads // group):
        mixes.append(
            pl.pallas_call(
                functools.partial(attend_kernel, steps, span, hd),
                grid=(1,),
                in_specs=[
                    smem,
                    columns(total, g),
                    columns(total, g),
                    columns(total, g),
                    columns(window, g),
                    columns(window, g),
                    pl.BlockSpec((total, wide), lambda i: (0, 0)),
                ],
                out_specs=pl.BlockSpec((total, wide), lambda i: (0, 0)),
                out_shape=jax.ShapeDtypeStruct((total, wide), bf16),
                compiler_params=params,
                name=f"attend_{g}",
            )(begins, q, k, v, past_keys[0], past_values[0], applied[g])
        )
    mix = jnp.concatenate(mixes, axis=1)
    placed = [mix[:span]]
    for s in range(1, steps):
        placed.append(passed_along(mix[s * span : (s + 1) * span], "seq", s))
    reduced = []
    for part in placed:
        partial_value = jnp.dot(part, out_weight, preferred_element_type=f32).astype(bf16)
        reduced.append(
            lax.psum_scatter(partial_value, "head", scatter_dimension=1, tiled=True)
        )
    mixed = jnp.concatenate(reduced, axis=0)
    fast_out = jnp.concatenate([w for w, _ in sent], axis=0).astype(f32)
    mom_out = jnp.concatenate([m for _, m in sent], axis=0).astype(f32)
    return (mixed[None], fast_out[None], mom_out[None])


def solution(mesh):
    in_specs = (
        P("seq", None, "head"),
        P("seq", "head", None, None),
        P("seq", "head", None, None),
        P("head", None, None),
        P("seq", None, "head"),
        P("seq", None, "head"),
        P(None, "seq", "head"),
        P(None, "head"),
        P("head", None),
        P(),
    )
    out_specs = (P("seq", None, "head"), P("seq", "head", None, None), P("seq", "head", None, None))
    return jax.shard_map(body, mesh=mesh, in_specs=in_specs, out_specs=out_specs, check_vma=False)
```

```python
import functools
import math

import jax
import jax.numpy as jnp
from jax import lax
from jax.experimental import pallas as pl
from jax.experimental.pallas import tpu as pltpu
from jax.sharding import PartitionSpec as P

momentum_decay = 0.9
rate_scale = 0.3
epsilon = 1e-06
f32 = jnp.float32
bf16 = jnp.bfloat16


def passed_along(block, axis, distance):
    n = lax.axis_size(axis)
    return lax.ppermute(block, axis, [((i - distance) % n, i) for i in range(n)])


def unit_rows(matrix):
    matrix = matrix.astype(f32)
    return matrix * lax.rsqrt(jnp.mean(matrix * matrix, axis=-1, keepdims=True) + epsilon)


def mm(a, b, ca, cb):
    return lax.dot_general(a, b, (((ca,), (cb,)), ((), ())), preferred_element_type=f32)


def fast_kernel(steps, span, begins, q, k, v, rate, fast, mom, init, applied, fast_out, mom_out):
    group, hd, three = fast.shape
    hid = three // 3
    inv_bound = 1.0 / math.sqrt(hd)
    inv_hidden = 1.0 / math.sqrt(hid)
    for h in range(group):
        cols = slice(h * hd, (h + 1) * hd)
        w = fast[h]
        m = mom[h]
        for s in range(steps):
            rows = slice(s * span, (s + 1) * span)
            fresh = begins[s] > 0
            w = jnp.where(fresh, init[h].astype(f32), w)
            m = jnp.where(fresh, 0.0, m)
            wb = w.astype(bf16)
            up = wb[:, : 2 * hid]
            down = wb[:, 2 * hid :]
            xq = (unit_rows(q[rows, cols]) * inv_bound).astype(bf16)
            ab = mm(xq, up, 1, 0)
            a = ab[:, :hid]
            hq = (a * jax.nn.sigmoid(a) * ab[:, hid:]).astype(bf16)
            applied[rows, cols] = mm(hq, down, 1, 1) * inv_hidden
            y = (unit_rows(k[rows, cols]) * inv_bound).astype(bf16)
            ab = mm(y, up, 1, 0)
            a = ab[:, :hid]
            b = ab[:, hid:]
            sg = jax.nn.sigmoid(a)
            act = a * sg
            g = (-rate[rows, h : h + 1] * v[rows, cols].astype(f32)).astype(bf16)
            grad_down = mm(g, (act * b).astype(bf16), 0, 0) * inv_hidden
            e = mm(g, down, 1, 0) * inv_hidden
            da = (e * b * sg * (1.0 + a * (1.0 - sg))).astype(bf16)
            db = (e * act).astype(bf16)
            grad = jnp.concatenate([mm(y, da, 0, 0), mm(y, db, 0, 0), grad_down], axis=1)
            m = momentum_decay * m + grad
            w = w - m
            w = w * lax.rsqrt(jnp.mean(w * w, axis=0, keepdims=True) + epsilon)
        fast_out[h] = w.astype(bf16)
        mom_out[h] = m.astype(bf16)


def attend_kernel(steps, span, hd, begins, q, k, v, past_k, past_v, applied, mix):
    window = past_k.shape[0]
    blocks = window // span
    bound = math.sqrt(hd)
    for h in range(q.shape[1] // hd):
        cols = slice(h * hd, (h + 1) * hd)
        keys = []
        values = []
        ones = jnp.ones((span, 64), bf16)
        for c in range(blocks + steps):
            kr, vr, at = (past_k, past_v, c) if c < blocks else (k, v, c - blocks)
            rows = slice(at * span, (at + 1) * span)
            keys.append(unit_rows(kr[rows, cols]).astype(bf16))
            values.append(jnp.concatenate([vr[rows, cols], ones], axis=1))
        for s in range(steps):
            rows = slice(s * span, (s + 1) * span)
            qn = unit_rows(q[rows, cols]).astype(bf16)
            acc = jnp.zeros((span, hd + 64), f32)
            row = lax.broadcasted_iota(jnp.int32, (span, span), 0)
            col = lax.broadcasted_iota(jnp.int32, (span, span), 1)
            for c in range(s, s + blocks + 1):
                dead = jnp.int32(0)
                for t in range(max(0, c - blocks + 1), s + 1):
                    dead = jnp.maximum(dead, begins[t])
                shift = jnp.where(dead > 0, -1e30, -bound)
                p = jnp.exp(mm(qn, keys[c], 1, 1) * (1.0 / bound) + shift)
                if c == s:
                    p = jnp.where(col > row, p, 0.0)
                if c == s + blocks:
                    p = jnp.where(col <= row, p, 0.0)
                acc = acc + mm(p.astype(bf16), values[c], 1, 0)
            out = acc[:, :hd] / acc[:, hd : hd + 1]
            mix[rows, cols] = (out + applied[rows, cols]).astype(bf16)


def gathered_features(spans):
    n_head = lax.axis_size("head")
    mine = lax.axis_index("head")
    span, width = spans[0].shape
    features = jnp.zeros((span * len(spans), width * n_head), spans[0].dtype)
    for s, part in enumerate(spans):
        for d in range(n_head):
            got = part if d == 0 else passed_along(part, "head", d)
            owner = lax.rem(mine - d + n_head, n_head)
            features = lax.dynamic_update_slice(features, got, (s * span, owner * width))
    return features


def layer(
    tokens,
    fast_state,
    momentum,
    init_fast,
    past_keys,
    past_values,
    qkv_weight,
    rate_weight,
    out_weight,
    prompt_begins,
):
    n = lax.axis_size("seq")
    me = lax.axis_index("seq")
    steps = prompt_begins.shape[0]
    total = tokens.shape[1]
    span = total // steps
    window = past_keys.shape[1]
    heads, hd, three = fast_state.shape[1:]
    group = 2 if heads % 2 == 0 else heads
    wide = group * hd

    weights = lax.all_gather(qkv_weight, "seq", axis=1, tiled=True)
    spans = [tokens[0, :span]]
    for s in range(1, steps):
        spans.append(passed_along(tokens[0, s * span : (s + 1) * span], "seq", -s))
    features = gathered_features(spans)
    q, k, v = [
        jnp.dot(features, weights[c], preferred_element_type=f32).astype(bf16) for c in range(3)
    ]
    rates = (
        rate_scale
        * jax.nn.softplus(jnp.dot(features, rate_weight, preferred_element_type=f32))
    ).astype(bf16).astype(f32)
    begins = jnp.stack([prompt_begins[s, (me + s) % n] for s in range(steps)])

    smem = pl.BlockSpec(memory_space=pltpu.SMEM)

    def columns(rows, g):
        return pl.BlockSpec((rows, wide), lambda i, g=g: (0, g))

    def state(g):
        return pl.BlockSpec((None, group, hd, three), lambda i, g=g: (0, g, 0, 0))

    params = pltpu.CompilerParams(vmem_limit_bytes=58 * 1024 * 1024)
    applied = []
    sent = []
    for g in range(heads // group):
        a, w, m = pl.pallas_call(
            functools.partial(fast_kernel, steps, span),
            grid=(1,),
            in_specs=[
                smem,
                columns(total, g),
                columns(total, g),
                columns(total, g),
                pl.BlockSpec((None, total, group), lambda i, g=g: (g, 0, 0)),
                state(g),
                state(g),
                pl.BlockSpec((group, hd, three), lambda i, g=g: (g, 0, 0)),
            ],
            out_specs=[
                pl.BlockSpec((total, wide), lambda i: (0, 0)),
                pl.BlockSpec((group, hd, three), lambda i: (0, 0, 0)),
                pl.BlockSpec((group, hd, three), lambda i: (0, 0, 0)),
            ],
            out_shape=[
                jax.ShapeDtypeStruct((total, wide), f32),
                jax.ShapeDtypeStruct((group, hd, three), bf16),
                jax.ShapeDtypeStruct((group, hd, three), bf16),
            ],
            compiler_params=params,
        )(
            begins,
            q,
            k,
            v,
            rates.reshape(total, heads // group, group).transpose(1, 0, 2),
            fast_state,
            momentum,
            init_fast,
        )
        applied.append(a)
        sent.append((passed_along(w, "seq", steps - 1), passed_along(m, "seq", steps - 1)))

    mixes = []
    for g in range(heads // group):
        mixes.append(
            pl.pallas_call(
                functools.partial(attend_kernel, steps, span, hd),
                grid=(1,),
                in_specs=[
                    smem,
                    columns(total, g),
                    columns(total, g),
                    columns(total, g),
                    columns(window, g),
                    columns(window, g),
                    pl.BlockSpec((total, wide), lambda i: (0, 0)),
                ],
                out_specs=pl.BlockSpec((total, wide), lambda i: (0, 0)),
                out_shape=jax.ShapeDtypeStruct((total, wide), bf16),
                compiler_params=params,
            )(begins, q, k, v, past_keys[0], past_values[0], applied[g])
        )
    mix = jnp.concatenate(mixes, axis=1)
    placed = [mix[:span]]
    for s in range(1, steps):
        placed.append(passed_along(mix[s * span : (s + 1) * span], "seq", s))
    reduced = []
    for part in placed:
        partial_value = jnp.dot(part, out_weight, preferred_element_type=f32).astype(bf16)
        reduced.append(
            lax.psum_scatter(partial_value, "head", scatter_dimension=1, tiled=True)
        )
    mixed = jnp.concatenate(reduced, axis=0)
    fast_out = jnp.concatenate([w for w, _ in sent], axis=0).astype(f32)
    mom_out = jnp.concatenate([m for _, m in sent], axis=0).astype(f32)
    return (mixed[None], fast_out[None], mom_out[None])


def solution(mesh):
    in_specs = (
        P("seq", None, "head"),
        P("seq", "head", None, None),
        P("seq", "head", None, None),
        P("head", None, None),
        P("seq", None, "head"),
        P("seq", None, "head"),
        P(None, "seq", "head"),
        P(None, "head"),
        P("head", None),
        P(),
    )
    out_specs = (P("seq", None, "head"), P("seq", "head", None, None), P("seq", "head", None, None))
    return jax.shard_map(layer, mesh=mesh, in_specs=in_specs, out_specs=out_specs, check_vma=False)
```

```python
import functools
import math

import jax
import jax.numpy as jnp
from jax import lax
from jax.experimental import pallas as pl
from jax.experimental.pallas import tpu as pltpu
from jax.sharding import PartitionSpec as P

momentum_decay = 0.9
rate_scale = 0.3
epsilon = 1e-06
f32 = jnp.float32
bf16 = jnp.bfloat16


def passed_along(block, axis, distance):
    n = lax.axis_size(axis)
    return lax.ppermute(block, axis, [((i - distance) % n, i) for i in range(n)])


def unit_rows(matrix):
    matrix = matrix.astype(f32)
    return matrix * lax.rsqrt(jnp.mean(matrix * matrix, axis=-1, keepdims=True) + epsilon)


def mm(a, b, ca, cb):
    return lax.dot_general(a, b, (((ca,), (cb,)), ((), ())), preferred_element_type=f32)


def fast_kernel(steps, span, begins, k, v, rate, fast, mom, init, used, fast_out, mom_out):
    group, hd, three = fast.shape
    hid = three // 3
    inv_bound = 1.0 / math.sqrt(hd)
    inv_hidden = 1.0 / math.sqrt(hid)
    for h in range(group):
        cols = slice(h * hd, (h + 1) * hd)
        w = fast[h]
        m = mom[h]
        for s in range(steps):
            rows = slice(s * span, (s + 1) * span)
            fresh = begins[s] > 0
            w = jnp.where(fresh, init[h].astype(f32), w)
            m = jnp.where(fresh, 0.0, m)
            wb = w.astype(bf16)
            up = wb[:, : 2 * hid]
            down = wb[:, 2 * hid :]
            used[s, h] = wb
            y = (unit_rows(k[rows, cols]) * inv_bound).astype(bf16)
            ab = mm(y, up, 1, 0)
            a = ab[:, :hid]
            b = ab[:, hid:]
            sg = jax.nn.sigmoid(a)
            act = a * sg
            g = (-rate[rows, h : h + 1] * v[rows, cols].astype(f32)).astype(bf16)
            grad_down = mm(g, (act * b).astype(bf16), 0, 0) * inv_hidden
            e = mm(g, down, 1, 0) * inv_hidden
            da = (e * b * sg * (1.0 + a * (1.0 - sg))).astype(bf16)
            db = (e * act).astype(bf16)
            grad = jnp.concatenate([mm(y, da, 0, 0), mm(y, db, 0, 0), grad_down], axis=1)
            m = momentum_decay * m + grad
            w = w - m
            w = w * lax.rsqrt(jnp.mean(w * w, axis=0, keepdims=True) + epsilon)
        fast_out[h] = w.astype(bf16)
        mom_out[h] = m.astype(bf16)


def attend_kernel(steps, span, hd, begins, q, k, v, past_k, past_v, used, mix):
    window = past_k.shape[0]
    blocks = window // span
    bound = math.sqrt(hd)
    hid = used.shape[3] // 3
    inv_hidden = 1.0 / math.sqrt(hid)
    for h in range(q.shape[1] // hd):
        cols = slice(h * hd, (h + 1) * hd)
        keys = []
        values = []
        ones = jnp.ones((span, 64), bf16)
        for c in range(blocks + steps):
            kr, vr, at = (past_k, past_v, c) if c < blocks else (k, v, c - blocks)
            rows = slice(at * span, (at + 1) * span)
            keys.append(unit_rows(kr[rows, cols]).astype(bf16))
            values.append(jnp.concatenate([vr[rows, cols], ones], axis=1))
        for s in range(steps):
            rows = slice(s * span, (s + 1) * span)
            qf = unit_rows(q[rows, cols])
            qn = qf.astype(bf16)
            xq = (qf * (1.0 / bound)).astype(bf16)
            ab = mm(xq, used[s, h, :, : 2 * hid], 1, 0)
            a = ab[:, :hid]
            hq = (a * jax.nn.sigmoid(a) * ab[:, hid:]).astype(bf16)
            applied = mm(hq, used[s, h, :, 2 * hid :], 1, 1) * inv_hidden
            acc = jnp.zeros((span, hd + 64), f32)
            row = lax.broadcasted_iota(jnp.int32, (span, span), 0)
            col = lax.broadcasted_iota(jnp.int32, (span, span), 1)
            for c in range(s, s + blocks + 1):
                dead = jnp.int32(0)
                for t in range(max(0, c - blocks + 1), s + 1):
                    dead = jnp.maximum(dead, begins[t])
                shift = jnp.where(dead > 0, -1e30, -bound)
                p = jnp.exp(mm(qn, keys[c], 1, 1) * (1.0 / bound) + shift)
                if c == s:
                    p = jnp.where(col > row, p, 0.0)
                if c == s + blocks:
                    p = jnp.where(col <= row, p, 0.0)
                acc = acc + mm(p.astype(bf16), values[c], 1, 0)
            out = acc[:, :hd] / acc[:, hd : hd + 1]
            mix[rows, cols] = (out + applied).astype(bf16)


def grid_of(n):
    across = 2 if n % 2 == 0 else 1
    up = 2 if n % (2 * across) == 0 else 1
    return (n // (across * up), up, across)


def gather_kernel(dims, w, out, send_sem, recv_sem, own_sem):
    size_z, size_y, size_x = dims
    me = lax.axis_index("seq")
    x = lax.rem(me, size_x)
    y = lax.rem(me // size_x, size_y)
    z = me // (size_x * size_y)

    def slot(dz, dy, dx):
        return (
            lax.rem(z + dz, size_z) * (size_y * size_x)
            + lax.rem(y + dy, size_y) * size_x
            + lax.rem(x + dx, size_x)
        )

    def held(dz, dy, dx):
        return slot((size_z - dz) % size_z, (size_y - dy) % size_y, (size_x - dx) % size_x)

    peers = [slot(d, 0, 0) for d in range(1, size_z)]
    peers += [slot(0, d, 0) for d in range(1, size_y)]
    peers += [slot(0, 0, d) for d in range(1, size_x)]
    barrier = pltpu.get_barrier_semaphore()
    for peer in peers:
        pl.semaphore_signal(
            barrier, inc=1, device_id={"seq": peer}, device_id_type=pl.DeviceIdType.MESH
        )
    pl.semaphore_wait(barrier, len(peers))

    parts = w.shape[0] - 1
    orders = ("zxy", "zyx")
    copies = [{} for _ in range(parts)]

    def send(part, item, axis, d):
        step = dict(zip("zyx", item))
        step[axis] = d
        lands = (step["z"], step["y"], step["x"])
        index = len(copies[part])
        source = held(*item)
        copy = pltpu.make_async_remote_copy(
            src_ref=w.at[part + 1] if item == (0, 0, 0) else out.at[part, source],
            dst_ref=out.at[part, source],
            send_sem=send_sem.at[part, index],
            recv_sem=recv_sem.at[part, index],
            device_id={"seq": slot(*[d if a == axis else 0 for a in "zyx"])},
            device_id_type=pl.DeviceIdType.MESH,
        )
        copy.start()
        copies[part][lands] = copy

    reach = {"z": size_z, "y": size_y, "x": size_x}

    def spread(part, item, axis):
        for d in range(1, reach[axis]):
            send(part, item, axis, d)

    own = [
        pltpu.make_async_copy(w.at[part + 1], out.at[part, me], own_sem.at[part])
        for part in range(parts)
    ]
    for part in range(parts):
        spread(part, (0, 0, 0), "z")
    for dz in range(size_z):
        for part in range(parts):
            if dz > 0:
                copies[part][(dz, 0, 0)].wait_recv()
            spread(part, (dz, 0, 0), orders[part][1])
        for part in range(parts):
            spread(part, (dz, 0, 0), orders[part][2])
    for copy in own:
        copy.start()
    for dz in range(size_z):
        for part in range(parts):
            axis = orders[part][1]
            for d in range(1, reach[axis]):
                item = tuple(dz if a == "z" else d if a == axis else 0 for a in "zyx")
                copies[part][item].wait_recv()
                spread(part, item, orders[part][2])
    for part in range(parts):
        last = "zyx".index(orders[part][2])
        for item, copy in copies[part].items():
            copy.wait_send()
            if item[last] > 0:
                copy.wait_recv()
    for copy in own:
        copy.wait()


def gathered_rows(weight):
    n = lax.axis_size("seq")
    three, rows, columns = weight.shape
    out = pl.pallas_call(
        functools.partial(gather_kernel, grid_of(n)),
        in_specs=[pl.BlockSpec(memory_space=pl.ANY)],
        out_specs=pl.BlockSpec(memory_space=pl.ANY),
        out_shape=jax.ShapeDtypeStruct((three - 1, n, rows, columns), weight.dtype),
        scratch_shapes=[
            pltpu.SemaphoreType.DMA((three - 1, n - 1)),
            pltpu.SemaphoreType.DMA((three - 1, n - 1)),
            pltpu.SemaphoreType.DMA((three - 1,)),
        ],
        compiler_params=pltpu.CompilerParams(collective_id=0, has_side_effects=True),
        name="gather_kv",
    )(weight)
    return out.reshape(three - 1, n * rows, columns)


def gathered_features(spans):
    n_head = lax.axis_size("head")
    mine = lax.axis_index("head")
    span, width = spans[0].shape
    features = jnp.zeros((span * len(spans), width * n_head), spans[0].dtype)
    for s, part in enumerate(spans):
        for d in range(n_head):
            got = part if d == 0 else passed_along(part, "head", d)
            owner = lax.rem(mine - d + n_head, n_head)
            features = lax.dynamic_update_slice(features, got, (s * span, owner * width))
    return features


def layer(
    tokens,
    fast_state,
    momentum,
    init_fast,
    past_keys,
    past_values,
    qkv_weight,
    rate_weight,
    out_weight,
    prompt_begins,
):
    n = lax.axis_size("seq")
    me = lax.axis_index("seq")
    steps = prompt_begins.shape[0]
    total = tokens.shape[1]
    span = total // steps
    window = past_keys.shape[1]
    heads, hd, three = fast_state.shape[1:]
    group = 2 if heads % 2 == 0 else heads
    wide = group * hd

    key_value = gathered_rows(qkv_weight)
    later, key_value = lax.optimization_barrier((qkv_weight[0], key_value))
    query_weight = lax.all_gather(later, "seq", axis=0, tiled=True)
    spans = [tokens[0, :span]]
    for s in range(1, steps):
        spans.append(passed_along(tokens[0, s * span : (s + 1) * span], "seq", -s))
    features = gathered_features(spans)
    k, v = [
        jnp.dot(features, key_value[c], preferred_element_type=f32).astype(bf16)
        for c in range(2)
    ]
    q = jnp.dot(features, query_weight, preferred_element_type=f32).astype(bf16)
    rates = (
        rate_scale
        * jax.nn.softplus(jnp.dot(features, rate_weight, preferred_element_type=f32))
    ).astype(bf16).astype(f32)
    begins = jnp.stack([prompt_begins[s, (me + s) % n] for s in range(steps)])

    smem = pl.BlockSpec(memory_space=pltpu.SMEM)

    def columns(rows, g):
        return pl.BlockSpec((rows, wide), lambda i, g=g: (0, g))

    def state(g):
        return pl.BlockSpec((None, group, hd, three), lambda i, g=g: (0, g, 0, 0))

    params = pltpu.CompilerParams(vmem_limit_bytes=58 * 1024 * 1024)
    applied = []
    sent = []
    for g in range(heads // group):
        a, w, m = pl.pallas_call(
            functools.partial(fast_kernel, steps, span),
            grid=(1,),
            in_specs=[
                smem,
                columns(total, g),
                columns(total, g),
                pl.BlockSpec((None, total, group), lambda i, g=g: (g, 0, 0)),
                state(g),
                state(g),
                pl.BlockSpec((group, hd, three), lambda i, g=g: (g, 0, 0)),
            ],
            out_specs=[
                pl.BlockSpec((steps, group, hd, three), lambda i: (0, 0, 0, 0)),
                pl.BlockSpec((group, hd, three), lambda i: (0, 0, 0)),
                pl.BlockSpec((group, hd, three), lambda i: (0, 0, 0)),
            ],
            out_shape=[
                jax.ShapeDtypeStruct((steps, group, hd, three), bf16),
                jax.ShapeDtypeStruct((group, hd, three), bf16),
                jax.ShapeDtypeStruct((group, hd, three), bf16),
            ],
            compiler_params=params,
        )(
            begins,
            k,
            v,
            rates.reshape(total, heads // group, group).transpose(1, 0, 2),
            fast_state,
            momentum,
            init_fast,
        )
        applied.append(a)
        sent.append((passed_along(w, "seq", steps - 1), passed_along(m, "seq", steps - 1)))

    mixes = []
    for g in range(heads // group):
        mixes.append(
            pl.pallas_call(
                functools.partial(attend_kernel, steps, span, hd),
                grid=(1,),
                in_specs=[
                    smem,
                    columns(total, g),
                    columns(total, g),
                    columns(total, g),
                    columns(window, g),
                    columns(window, g),
                    pl.BlockSpec((steps, group, hd, three), lambda i: (0, 0, 0, 0)),
                ],
                out_specs=pl.BlockSpec((total, wide), lambda i: (0, 0)),
                out_shape=jax.ShapeDtypeStruct((total, wide), bf16),
                compiler_params=params,
            )(begins, q, k, v, past_keys[0], past_values[0], applied[g])
        )
    mix = jnp.concatenate(mixes, axis=1)
    placed = [mix[:span]]
    for s in range(1, steps):
        placed.append(passed_along(mix[s * span : (s + 1) * span], "seq", s))
    reduced = []
    for part in placed:
        partial_value = jnp.dot(part, out_weight, preferred_element_type=f32).astype(bf16)
        reduced.append(
            lax.psum_scatter(partial_value, "head", scatter_dimension=1, tiled=True)
        )
    mixed = jnp.concatenate(reduced, axis=0)
    fast_out = jnp.concatenate([w for w, _ in sent], axis=0).astype(f32)
    mom_out = jnp.concatenate([m for _, m in sent], axis=0).astype(f32)
    return (mixed[None], fast_out[None], mom_out[None])


def solution(mesh):
    in_specs = (
        P("seq", None, "head"),
        P("seq", "head", None, None),
        P("seq", "head", None, None),
        P("head", None, None),
        P("seq", None, "head"),
        P("seq", None, "head"),
        P(None, "seq", "head"),
        P(None, "head"),
        P("head", None),
        P(),
    )
    out_specs = (P("seq", None, "head"), P("seq", "head", None, None), P("seq", "head", None, None))
    return jax.shard_map(layer, mesh=mesh, in_specs=in_specs, out_specs=out_specs, check_vma=False)
```

```python
import functools
import math

import jax
import jax.numpy as jnp
from jax import lax
from jax.experimental import pallas as pl
from jax.experimental.pallas import tpu as pltpu
from jax.sharding import PartitionSpec as P

momentum_decay = 0.9
rate_scale = 0.3
epsilon = 1e-06
f32 = jnp.float32
bf16 = jnp.bfloat16


def passed_along(block, axis, distance):
    n = lax.axis_size(axis)
    return lax.ppermute(block, axis, [((i - distance) % n, i) for i in range(n)])


def unit_rows(matrix):
    matrix = matrix.astype(f32)
    return matrix * lax.rsqrt(jnp.mean(matrix * matrix, axis=-1, keepdims=True) + epsilon)


def mm(a, b, ca, cb):
    return lax.dot_general(a, b, (((ca,), (cb,)), ((), ())), preferred_element_type=f32)


def fast_kernel(steps, span, begins, k, v, rate, fast, mom, init, used, fast_out, mom_out):
    group, hd, three = fast.shape
    hid = three // 3
    inv_bound = 1.0 / math.sqrt(hd)
    inv_hidden = 1.0 / math.sqrt(hid)
    for h in range(group):
        cols = slice(h * hd, (h + 1) * hd)
        w = fast[h]
        m = mom[h]
        for s in range(steps):
            rows = slice(s * span, (s + 1) * span)
            fresh = begins[s] > 0
            w = jnp.where(fresh, init[h].astype(f32), w)
            m = jnp.where(fresh, 0.0, m)
            wb = w.astype(bf16)
            up = wb[:, : 2 * hid]
            down = wb[:, 2 * hid :]
            used[s, h] = wb
            y = (unit_rows(k[rows, cols]) * inv_bound).astype(bf16)
            ab = mm(y, up, 1, 0)
            a = ab[:, :hid]
            b = ab[:, hid:]
            sg = jax.nn.sigmoid(a)
            act = a * sg
            g = (-rate[rows, h : h + 1] * v[rows, cols].astype(f32)).astype(bf16)
            grad_down = mm(g, (act * b).astype(bf16), 0, 0) * inv_hidden
            e = mm(g, down, 1, 0) * inv_hidden
            da = (e * b * sg * (1.0 + a * (1.0 - sg))).astype(bf16)
            db = (e * act).astype(bf16)
            grad = jnp.concatenate([mm(y, da, 0, 0), mm(y, db, 0, 0), grad_down], axis=1)
            m = momentum_decay * m + grad
            w = w - m
            w = w * lax.rsqrt(jnp.mean(w * w, axis=0, keepdims=True) + epsilon)
        fast_out[h] = w.astype(bf16)
        mom_out[h] = m.astype(bf16)


def attend_kernel(steps, span, hd, begins, q, k, v, past_k, past_v, used, mix):
    window = past_k.shape[0]
    blocks = window // span
    bound = math.sqrt(hd)
    hid = used.shape[3] // 3
    inv_hidden = 1.0 / math.sqrt(hid)
    for h in range(q.shape[1] // hd):
        cols = slice(h * hd, (h + 1) * hd)
        keys = []
        values = []
        ones = jnp.ones((span, 64), bf16)
        for c in range(blocks + steps):
            kr, vr, at = (past_k, past_v, c) if c < blocks else (k, v, c - blocks)
            rows = slice(at * span, (at + 1) * span)
            keys.append(unit_rows(kr[rows, cols]).astype(bf16))
            values.append(jnp.concatenate([vr[rows, cols], ones], axis=1))
        for s in range(steps):
            rows = slice(s * span, (s + 1) * span)
            qf = unit_rows(q[rows, cols])
            qn = qf.astype(bf16)
            xq = (qf * (1.0 / bound)).astype(bf16)
            ab = mm(xq, used[s, h, :, : 2 * hid], 1, 0)
            a = ab[:, :hid]
            hq = (a * jax.nn.sigmoid(a) * ab[:, hid:]).astype(bf16)
            applied = mm(hq, used[s, h, :, 2 * hid :], 1, 1) * inv_hidden
            acc = jnp.zeros((span, hd + 64), f32)
            row = lax.broadcasted_iota(jnp.int32, (span, span), 0)
            col = lax.broadcasted_iota(jnp.int32, (span, span), 1)
            for c in range(s, s + blocks + 1):
                dead = jnp.int32(0)
                for t in range(max(0, c - blocks + 1), s + 1):
                    dead = jnp.maximum(dead, begins[t])
                shift = jnp.where(dead > 0, -1e30, -bound)
                p = jnp.exp(mm(qn, keys[c], 1, 1) * (1.0 / bound) + shift)
                if c == s:
                    p = jnp.where(col > row, p, 0.0)
                if c == s + blocks:
                    p = jnp.where(col <= row, p, 0.0)
                acc = acc + mm(p.astype(bf16), values[c], 1, 0)
            out = acc[:, :hd] / acc[:, hd : hd + 1]
            mix[rows, cols] = (out + applied).astype(bf16)


def grid_of(n):
    across = 2 if n % 2 == 0 else 1
    up = 2 if n % (2 * across) == 0 else 1
    return (n // (across * up), up, across)


def gather_kernel(dims, w, out, send_sem, recv_sem, own_sem):
    size_z, size_y, size_x = dims
    me = lax.axis_index("seq")
    x = lax.rem(me, size_x)
    y = lax.rem(me // size_x, size_y)
    z = me // (size_x * size_y)

    def slot(dz, dy, dx):
        return (
            lax.rem(z + dz, size_z) * (size_y * size_x)
            + lax.rem(y + dy, size_y) * size_x
            + lax.rem(x + dx, size_x)
        )

    def held(dz, dy, dx):
        return slot((size_z - dz) % size_z, (size_y - dy) % size_y, (size_x - dx) % size_x)

    peers = [slot(d, 0, 0) for d in range(1, size_z)]
    peers += [slot(0, d, 0) for d in range(1, size_y)]
    peers += [slot(0, 0, d) for d in range(1, size_x)]
    barrier = pltpu.get_barrier_semaphore()
    for peer in peers:
        pl.semaphore_signal(
            barrier, inc=1, device_id={"seq": peer}, device_id_type=pl.DeviceIdType.MESH
        )
    pl.semaphore_wait(barrier, len(peers))

    parts = w.shape[0] - 1
    orders = ("zxy", "zyx")
    copies = [{} for _ in range(parts)]

    def send(part, item, axis, d):
        step = dict(zip("zyx", item))
        step[axis] = d
        lands = (step["z"], step["y"], step["x"])
        index = len(copies[part])
        source = held(*item)
        copy = pltpu.make_async_remote_copy(
            src_ref=w.at[part + 1] if item == (0, 0, 0) else out.at[part, source],
            dst_ref=out.at[part, source],
            send_sem=send_sem.at[part, index],
            recv_sem=recv_sem.at[part, index],
            device_id={"seq": slot(*[d if a == axis else 0 for a in "zyx"])},
            device_id_type=pl.DeviceIdType.MESH,
        )
        copy.start()
        copies[part][lands] = copy

    reach = {"z": size_z, "y": size_y, "x": size_x}

    def spread(part, item, axis):
        for d in range(1, reach[axis]):
            send(part, item, axis, d)

    own = [
        pltpu.make_async_copy(w.at[part + 1], out.at[part, me], own_sem.at[part])
        for part in range(parts)
    ]
    for part in range(parts):
        spread(part, (0, 0, 0), "z")
    for dz in range(size_z):
        for part in range(parts):
            if dz > 0:
                copies[part][(dz, 0, 0)].wait_recv()
            spread(part, (dz, 0, 0), orders[part][1])
        for part in range(parts):
            spread(part, (dz, 0, 0), orders[part][2])
    for copy in own:
        copy.start()
    for dz in range(size_z):
        for part in range(parts):
            axis = orders[part][1]
            for d in range(1, reach[axis]):
                item = tuple(dz if a == "z" else d if a == axis else 0 for a in "zyx")
                copies[part][item].wait_recv()
                spread(part, item, orders[part][2])
    for part in range(parts):
        last = "zyx".index(orders[part][2])
        for item, copy in copies[part].items():
            copy.wait_send()
            if item[last] > 0:
                copy.wait_recv()
    for copy in own:
        copy.wait()


def gathered_rows(weight):
    n = lax.axis_size("seq")
    three, rows, columns = weight.shape
    out = pl.pallas_call(
        functools.partial(gather_kernel, grid_of(n)),
        in_specs=[pl.BlockSpec(memory_space=pl.ANY)],
        out_specs=pl.BlockSpec(memory_space=pl.ANY),
        out_shape=jax.ShapeDtypeStruct((three - 1, n, rows, columns), weight.dtype),
        scratch_shapes=[
            pltpu.SemaphoreType.DMA((three - 1, n - 1)),
            pltpu.SemaphoreType.DMA((three - 1, n - 1)),
            pltpu.SemaphoreType.DMA((three - 1,)),
        ],
        compiler_params=pltpu.CompilerParams(collective_id=0, has_side_effects=True),
        name="gather_kv",
    )(weight)
    return out.reshape(three - 1, n * rows, columns)


def gathered_features(spans):
    n_head = lax.axis_size("head")
    mine = lax.axis_index("head")
    span, width = spans[0].shape
    features = jnp.zeros((span * len(spans), width * n_head), spans[0].dtype)
    for s, part in enumerate(spans):
        for d in range(n_head):
            got = part if d == 0 else passed_along(part, "head", d)
            owner = lax.rem(mine - d + n_head, n_head)
            features = lax.dynamic_update_slice(features, got, (s * span, owner * width))
    return features


def layer(
    tokens,
    fast_state,
    momentum,
    init_fast,
    past_keys,
    past_values,
    qkv_weight,
    rate_weight,
    out_weight,
    prompt_begins,
):
    n = lax.axis_size("seq")
    me = lax.axis_index("seq")
    steps = prompt_begins.shape[0]
    total = tokens.shape[1]
    span = total // steps
    window = past_keys.shape[1]
    heads, hd, three = fast_state.shape[1:]
    group = 2 if heads % 2 == 0 else heads
    wide = group * hd

    key_value = gathered_rows(qkv_weight)
    later, key_value = lax.optimization_barrier((qkv_weight[0], key_value))
    query_weight = lax.all_gather(later, "seq", axis=0, tiled=True)
    spans = [tokens[0, :span]]
    for s in range(1, steps):
        spans.append(passed_along(tokens[0, s * span : (s + 1) * span], "seq", -s))
    features = gathered_features(spans)
    k, v = [
        jnp.dot(features, key_value[c], preferred_element_type=f32).astype(bf16)
        for c in range(2)
    ]
    rates = (
        rate_scale
        * jax.nn.softplus(jnp.dot(features, rate_weight, preferred_element_type=f32))
    ).astype(bf16).astype(f32)
    begins = jnp.stack([prompt_begins[s, (me + s) % n] for s in range(steps)])

    smem = pl.BlockSpec(memory_space=pltpu.SMEM)

    def columns(rows, g):
        return pl.BlockSpec((rows, wide), lambda i, g=g: (0, g))

    def state(g):
        return pl.BlockSpec((None, group, hd, three), lambda i, g=g: (0, g, 0, 0))

    params = pltpu.CompilerParams(vmem_limit_bytes=58 * 1024 * 1024)
    applied = []
    sent = []
    kept = []
    for g in range(heads // group):
        a, w, m = pl.pallas_call(
            functools.partial(fast_kernel, steps, span),
            grid=(1,),
            in_specs=[
                smem,
                columns(total, g),
                columns(total, g),
                pl.BlockSpec((None, total, group), lambda i, g=g: (g, 0, 0)),
                state(g),
                state(g),
                pl.BlockSpec((group, hd, three), lambda i, g=g: (g, 0, 0)),
            ],
            out_specs=[
                pl.BlockSpec((steps, group, hd, three), lambda i: (0, 0, 0, 0)),
                pl.BlockSpec((group, hd, three), lambda i: (0, 0, 0)),
                pl.BlockSpec((group, hd, three), lambda i: (0, 0, 0)),
            ],
            out_shape=[
                jax.ShapeDtypeStruct((steps, group, hd, three), bf16),
                jax.ShapeDtypeStruct((group, hd, three), bf16),
                jax.ShapeDtypeStruct((group, hd, three), bf16),
            ],
            compiler_params=params,
        )(
            begins,
            k,
            v,
            rates.reshape(total, heads // group, group).transpose(1, 0, 2),
            fast_state,
            momentum,
            init_fast,
        )
        applied.append(a)
        w, query_weight = lax.optimization_barrier((w, query_weight))
        sent.append(passed_along(w, "seq", steps - 1))
        kept.append(m)

    q = jnp.dot(features, query_weight, preferred_element_type=f32).astype(bf16)
    mixes = []
    for g in range(heads // group):
        mixes.append(
            pl.pallas_call(
                functools.partial(attend_kernel, steps, span, hd),
                grid=(1,),
                in_specs=[
                    smem,
                    columns(total, g),
                    columns(total, g),
                    columns(total, g),
                    columns(window, g),
                    columns(window, g),
                    pl.BlockSpec((steps, group, hd, three), lambda i: (0, 0, 0, 0)),
                ],
                out_specs=pl.BlockSpec((total, wide), lambda i: (0, 0)),
                out_shape=jax.ShapeDtypeStruct((total, wide), bf16),
                compiler_params=params,
            )(begins, q, k, v, past_keys[0], past_values[0], applied[g])
        )
    mix = jnp.concatenate(mixes, axis=1)
    placed = [mix[:span]]
    for s in range(1, steps):
        placed.append(passed_along(mix[s * span : (s + 1) * span], "seq", s))
    *kept, placed[-1] = lax.optimization_barrier((*kept, placed[-1]))
    moved = [passed_along(m, "seq", steps - 1) for m in kept]
    reduced = []
    for part in placed:
        partial_value = jnp.dot(part, out_weight, preferred_element_type=f32).astype(bf16)
        reduced.append(
            lax.psum_scatter(partial_value, "head", scatter_dimension=1, tiled=True)
        )
    mixed = jnp.concatenate(reduced, axis=0)
    fast_out = jnp.concatenate(sent, axis=0).astype(f32)
    mom_out = jnp.concatenate(moved, axis=0).astype(f32)
    return (mixed[None], fast_out[None], mom_out[None])


def solution(mesh):
    in_specs = (
        P("seq", None, "head"),
        P("seq", "head", None, None),
        P("seq", "head", None, None),
        P("head", None, None),
        P("seq", None, "head"),
        P("seq", None, "head"),
        P(None, "seq", "head"),
        P(None, "head"),
        P("head", None),
        P(),
    )
    out_specs = (P("seq", None, "head"), P("seq", "head", None, None), P("seq", "head", None, None))
    return jax.shard_map(layer, mesh=mesh, in_specs=in_specs, out_specs=out_specs, check_vma=False)
```
